32 devices in a mesh: shot: 2 (over x), strip: 16 (over z, y, core).
Axes of the slice: x: 2, y: 2, z: 4, core: 2. Of those that a mesh axis runs over, the one named last changes fastest.
Arguments:
- waves: float32 [2, 2, 8, 512, 512], P(None, None, 'shot', 'strip'), parts along dimension 2, may hold values from -6 to 6
- levels: int32 [512, 512], P('strip'), may hold values from 0 to 4
- coeffs: float32 [2, 4, 5, 17], replicated, may hold values from -0.7 to 0.7
- angles: float32 [4, 5], replicated, may hold values from -3.140625 to 3.140625
- order: int32 [8], P('shot'), parts along dimension 0, may hold values from 0 to 3, each once
Outputs:
- waves_out: float32 [2, 2, 8, 512, 512], P(None, None, 'shot', 'strip'), parts along dimension 2
- image: float32 [4, 512, 512], P('shot', 'strip'), parts along dimension 0
The draws below stay inside these ranges and needn't reach their ends.
There are 2 independent parts, one for each index of `shot`. The reference program is written for one: setup_inputs(seed, part) draws one part's arguments, and reference() takes and returns one part's arrays. A program takes and returns all parts, laid end to end along the dimension named above; an argument that names none is the same for every part. Nothing has to cross between parts.
Inputs may be any that keep to these rules, and one draw needn't show every extreme that they name: order names every table row once.
All inputs are finite; a program needn't handle non-finite values.
Results may differ from the reference program's by a relative error of at most 0.00013.
Values sent between devices are 32-bit elements; how exact they have to be, the bound alone decides.
A program may use at most 64 MiB of HBM per device.

```python
import jax
import jax.numpy as jnp
from jax import lax

INLINE = 512
FREQ = 4
LEVELS = 5
TAPS = 17
STEPS = 2
CROSS = 512


def set_ends(array, key, least, top_value):
    longest = array.shape.index(max(array.shape))
    spots = []
    for shift in (0, 1):
        where = [jax.random.randint(jax.random.fold_in(key, axis), (), 0, length) for axis, length in enumerate(array.shape)]
        where[longest] = (where[longest] + shift) % array.shape[longest]
        spots.append(tuple(where))
    return array.at[spots[0]].set(least).at[spots[1]].set(top_value)


def steps_of(rng, dims, split, smallest, high):
    factor_of = 1.0
    for position, shards_of in split:
        heights = jax.random.uniform(jax.random.fold_in(jax.random.fold_in(rng, 6), position), (shards_of,), jnp.float32, smallest / len(split), high / len(split))
        factor_of = factor_of * jnp.repeat(jnp.exp(heights), dims[position] // shards_of).reshape((-1,) + (1,) * (len(dims) - 1 - position))
    return factor_of


def gaussian(rng, shape, scale, most, split=(), kind=jnp.bfloat16):
    entries = scale * jax.random.normal(rng, shape, jnp.float32)
    if split:
        entries = entries * steps_of(rng, shape, split, -0.22, 0.18)
    return jnp.clip(entries, -most, most).astype(kind)


def setup_inputs(seed: int = 0, part: int = 0) -> dict:
    key_of = jax.random.split(jax.random.key(seed), 6)
    part_keys = jax.random.split(jax.random.fold_in(key_of[5], part), 6)
    waves = gaussian(part_keys[0], (2, 2, FREQ, CROSS, INLINE), 1.0, 6.0, ((3, 16),), jnp.float32)
    levels = set_ends(jax.random.randint(key_of[1], (CROSS, INLINE), 0, LEVELS), jax.random.fold_in(key_of[1], 1), 0, LEVELS - 1).astype(jnp.int32)
    coeffs = gaussian(key_of[2], (2, FREQ, LEVELS, TAPS), 0.17, 0.7, (), jnp.float32)
    angles = jnp.clip(jax.random.uniform(key_of[3], (FREQ, LEVELS), jnp.float32, -3.140625, 3.140625), -3.140625, 3.140625)
    order = jax.random.permutation(part_keys[4], FREQ).astype(jnp.int32)
    return {"waves": waves, "levels": levels, "coeffs": coeffs, "angles": angles, "order": order}


def one_pass(field_real, field_imag, coef_table, levels, along_axis, conj_sign, half_taps):
    widths = [(0, 0), (0, 0), (0, 0)]
    widths[along_axis] = (half_taps, half_taps)
    pad_real = jnp.pad(field_real, widths)
    pad_imag = jnp.pad(field_imag, widths)
    out_length = field_real.shape[along_axis]
    acc_real = jnp.zeros(field_real.shape, jnp.float32)
    acc_imag = jnp.zeros(field_real.shape, jnp.float32)
    for tap_index in range(2 * half_taps + 1):
        shift_real = lax.slice_in_dim(pad_real, tap_index, tap_index + out_length, axis=along_axis)
        shift_imag = lax.slice_in_dim(pad_imag, tap_index, tap_index + out_length, axis=along_axis)
        coef_real = coef_table[0][:, levels, tap_index]
        coef_imag = coef_table[1][:, levels, tap_index] * conj_sign
        acc_real = acc_real + (coef_real * shift_real - coef_imag * shift_imag)
        acc_imag = acc_imag + (coef_real * shift_imag + coef_imag * shift_real)
    return acc_real, acc_imag


def reference(waves, levels, coeffs, angles, order):
    coef_table = coeffs[:, order]
    turn_table = angles[order]
    phase_angle = turn_table[:, levels]
    cosine = jnp.cos(phase_angle)
    sine_part = jnp.sin(phase_angle)
    half_taps = (coeffs.shape[3] - 1) // 2
    source_real, source_imag = waves[0, 0], waves[0, 1]
    receiver_real, receiver_imag = waves[1, 0], waves[1, 1]
    slabs = []
    for depth_step in range(STEPS):
        source_real, source_imag = (source_real * cosine - source_imag * sine_part,
                                    source_real * sine_part + source_imag * cosine)
        receiver_real, receiver_imag = (receiver_real * cosine + receiver_imag * sine_part,
                                        -receiver_real * sine_part + receiver_imag * cosine)
        for along_axis in (2, 1):
            source_real, source_imag = one_pass(source_real, source_imag, coef_table, levels, along_axis, 1.0, half_taps)
            receiver_real, receiver_imag = one_pass(receiver_real, receiver_imag, coef_table, levels, along_axis, -1.0, half_taps)
        slabs.append(jnp.sum(source_real * receiver_real + source_imag * receiver_imag, axis=0))
    waves_out = jnp.stack([jnp.stack([source_real, source_imag]), jnp.stack([receiver_real, receiver_imag])])
    return waves_out, jnp.stack(slabs)
```

```python
import functools

import jax
import jax.numpy as jnp
from jax import lax
from jax.experimental import pallas as pl
from jax.experimental.pallas import tpu as pltpu
from jax.sharding import PartitionSpec as P

STEPS = 2
LANES = 128
SUBS = 8
WIN = 16
MESH = pl.DeviceIdType.MESH


def split(v):
    high = v.astype(jnp.bfloat16)
    low = (v - high.astype(jnp.float32)).astype(jnp.bfloat16)
    return high, low


def pick(level, entries):
    out = entries[0]
    for i, entry in enumerate(entries[1:], 1):
        out = jnp.where(level == i, entry, out)
    return out


def filtered(table, parts, level):
    (hr, hi), (lr, li) = parts
    sums = jnp.dot(
        table, jnp.concatenate([hr, hi, lr, li, hr, hi], axis=0), preferred_element_type=jnp.float32
    )
    count = sums.shape[0] // (2 * WIN)
    return [
        pick(level, [sums[(2 * i + comp) * WIN : (2 * i + comp + 1) * WIN] for i in range(count)])
        for comp in range(2)
    ]


def kernel(
    sizes, waves_hbm, levels_hbm, coeffs_hbm, angles_hbm, order_hbm, out_ref, image_ref,
    order_ref, level_ref, coef_ref, angle_ref, load_sem,
    turned_ref, base_ref, turn_ref, table_ref, cos_ref, sin_ref,
    field_ref, part_ref, pass_ref, mid_ref, cross_ref, send_sem, recv_sem,
):
    freqs, rows, cells, levels, taps, strips = sizes
    half = taps // 2
    blocks = cells // LANES
    me = lax.axis_index("strip")
    has_low, has_high = me > 0, me < strips - 1

    small = [
        pltpu.make_async_copy(source, target, load_sem.at[i])
        for i, (source, target) in enumerate(
            ((coeffs_hbm, coef_ref), (angles_hbm, angle_ref), (levels_hbm, level_ref), (order_hbm, order_ref))
        )
    ]
    for load in small:
        load.start()

    def wave_load(f):
        return pltpu.make_async_copy(waves_hbm.at[:, :, f], field_ref.at[f], load_sem.at[4 + f])

    for f in range(freqs):
        wave_load(f).start()

    def neighbour(step):
        return {"strip": me + step}

    barrier = pltpu.get_barrier_semaphore()
    for there, step in ((has_low, -1), (has_high, 1)):

        @pl.when(there)
        def _():
            pl.semaphore_signal(barrier, inc=1, device_id=neighbour(step), device_id_type=MESH)

    lane = lax.broadcasted_iota(jnp.int32, (SUBS, LANES), 1)

    for there, first in ((has_low, 0), (has_high, rows + half)):

        @pl.when(jnp.logical_not(there))
        def _():
            for step in range(STEPS):

                @pl.loop(0, freqs)
                def _(f):
                    for field in range(2):
                        for comp in range(2):
                            mid_ref[step, f, field, comp, first : first + half, :] = jnp.zeros(
                                (half, cells), jnp.float32
                            )

    base_ref[...] = jnp.zeros_like(base_ref)
    small[0].wait()
    for comp in range(2):
        for level in range(levels):
            base_ref[comp, level, :, :taps] = coef_ref[comp, level]
    for level in range(levels):
        real, imag = base_ref[0, level], base_ref[1, level]
        for comp, (first, second) in enumerate(((real, -imag), (imag, real))):
            both = first + pltpu.roll(second, 2 * WIN, 1)
            base_ref[comp, level] = both + pltpu.roll(both, 4 * WIN, 1)

    small[1].wait()
    turn_ref[...] = jnp.zeros_like(turn_ref)
    angle = angle_ref[...]
    turn_ref[0, :, :levels] = jnp.cos(angle)
    turn_ref[1, :, :levels] = jnp.sin(angle)

    small[2].wait()
    small[3].wait()
    stacked = jnp.concatenate([level_ref[:, q * LANES : (q + 1) * LANES] for q in range(blocks)], axis=0)
    turned_ref[...] = stacked.T

    def prepare(f):
        row = pl.ds(order_ref[f], 1)
        for level in range(levels):
            for comp in range(2):
                line = jnp.broadcast_to(base_ref[comp, level, row, :], (WIN, LANES))
                high, low = split(pltpu.roll(line, 0, 1, stride=1, stride_axis=0))
                at = (2 * level + comp) * WIN
                table_ref[f, at : at + WIN, :LANES] = high
                table_ref[f, at : at + WIN, LANES:] = low[:, : 4 * WIN]
        for which, target in enumerate((cos_ref, sin_ref)):
            line = turn_ref[which, row, :]
            entries = [jnp.broadcast_to(line[:, i : i + 1], (SUBS, LANES)) for i in range(levels)]
            for top in range(0, rows, SUBS):
                for q in range(blocks):
                    level = level_ref[top : top + SUBS, q * LANES : (q + 1) * LANES]
                    target[f, top : top + SUBS, q * LANES : (q + 1) * LANES] = pick(level, entries)

    def inline_pass(step, f):
        cosine, sine = cos_ref[f], sin_ref[f]
        for field in range(2):
            real, imag = field_ref[f, field, 0], field_ref[f, field, 1]
            if step == 0 and field == 1:
                imag = -imag
            turned = (real * cosine - imag * sine, real * sine + imag * cosine)
            for comp in range(2):
                v = turned[comp]
                v = jnp.concatenate([v[:, q * LANES : (q + 1) * LANES] for q in range(blocks)], axis=0).T
                before = jnp.where(lane >= rows, pltpu.roll(v[LANES - half :], rows, 1), 0.0)
                after = jnp.where(lane < LANES - rows, pltpu.roll(v[:half], LANES - rows, 1), 0.0)
                for part, piece in enumerate(split(jnp.concatenate([before, v, after], axis=0))):
                    part_ref[part, comp, :, field * LANES : (field + 1) * LANES] = piece
        table = table_ref[f]
        for b in range(0, LANES, WIN):
            parts = [[part_ref[part, comp, b : b + 2 * WIN, :] for comp in range(2)] for part in range(2)]
            level = turned_ref[b : b + WIN, :]
            sums = filtered(table, parts, jnp.concatenate([level, level], axis=1))
            for comp in range(2):
                pass_ref[comp, b : b + WIN, :] = sums[comp]
        for field in range(2):
            for comp in range(2):
                v = pass_ref[comp, :, field * LANES : (field + 1) * LANES].T
                for q in range(blocks):
                    mid_ref[step, f, field, comp, half : half + rows, q * LANES : (q + 1) * LANES] = v[
                        q * rows : (q + 1) * rows
                    ]

    def cross_pass(step, f):
        last = step == STEPS - 1
        for field in range(2):
            for comp in range(2):
                for part, piece in enumerate(split(mid_ref[step, f, field, comp])):
                    cross_ref[part, field, comp] = piece
        table = table_ref[f]
        wide = 2 * LANES
        for b in range(0, rows, WIN):
            for x in range(0, cells, wide):
                at = (slice(b, b + WIN), slice(x, x + wide))
                level = level_ref[at]
                sums = []
                for field in range(2):
                    parts = [
                        [cross_ref[part, field, comp, b : b + 2 * WIN, x : x + wide] for comp in range(2)]
                        for part in range(2)
                    ]
                    sums.append(filtered(table, parts, level))
                (sr, si), (qr, qi) = sums
                for field in range(2):
                    for comp in range(2):
                        v = sums[field][comp]
                        if last:
                            out_ref[(field, comp, f) + at] = -v if field and comp else v
                        else:
                            field_ref[(f, field, comp) + at] = v
                image_ref[(step,) + at] += sr * qr - si * qi

    def halo_copy(step, f, side):
        source, target = ((half, rows + half), (rows, 0))[side]
        return pltpu.make_async_remote_copy(
            src_ref=mid_ref.at[step, f, :, :, pl.ds(source, half), :],
            dst_ref=mid_ref.at[step, f, :, :, pl.ds(target, half), :],
            send_sem=send_sem.at[step, f, side],
            recv_sem=recv_sem.at[step, f, side],
            device_id=neighbour((-1, 1)[side]),
            device_id_type=MESH,
        )

    def send(step, f):
        for side, there in enumerate((has_low, has_high)):

            @pl.when(there)
            def _():
                halo_copy(step, f, side).start()

    def receive(step, f):
        for side, there in ((1, has_low), (0, has_high)):

            @pl.when(there)
            def _():
                halo_copy(step, f, side).wait_recv()

    image_ref[...] = jnp.zeros_like(image_ref)

    prepare(0)
    wave_load(0).wait()
    inline_pass(0, 0)
    pl.semaphore_wait(barrier, has_low.astype(jnp.int32) + has_high.astype(jnp.int32))
    send(0, 0)

    @pl.loop(1, freqs)
    def _(f):
        prepare(f)
        wave_load(f).wait()
        inline_pass(0, f)
        send(0, f)

    @pl.loop(0, freqs)
    def _(f):
        receive(0, f)
        cross_pass(0, f)
        inline_pass(1, f)
        send(1, f)

    @pl.loop(0, freqs)
    def _(f):
        receive(1, f)
        cross_pass(1, f)

    for step in range(STEPS):

        @pl.loop(0, freqs)
        def _(f):
            for side, there in enumerate((has_low, has_high)):

                @pl.when(there)
                def _():
                    halo_copy(step, f, side).wait_send()


def store_kernel(waves_ref, image_ref, waves_hbm, image_hbm, sem):
    copies = [
        pltpu.make_async_copy(waves_ref, waves_hbm, sem.at[0]),
        pltpu.make_async_copy(image_ref, image_hbm, sem.at[1]),
    ]
    for copy in copies:
        copy.start()
    for copy in copies:
        copy.wait()


def on_device(strips, waves, levels, coeffs, angles, order):
    freqs, rows, cells = waves.shape[2:]
    level_count, taps = coeffs.shape[2:]
    half = taps // 2
    blocks = cells // LANES
    assert blocks * rows == LANES and rows % WIN == 0 and half == SUBS and taps == WIN + 1
    sizes = (freqs, rows, cells, level_count, taps, strips)
    table = (level_count * 2 * WIN, 6 * 2 * WIN)
    coeffs = jnp.transpose(coeffs, (0, 2, 1, 3))
    vmem, hbm = [pl.BlockSpec(memory_space=space) for space in (pltpu.VMEM, pltpu.HBM)]
    f32, bf16 = jnp.float32, jnp.bfloat16
    image_shape = (STEPS, rows, cells)
    span = rows + 2 * half
    shape, levels_shape, coeffs_shape, angles_shape = waves.shape, levels.shape, coeffs.shape, angles.shape
    waves, levels, coeffs, angles, order = [
        pltpu.with_memory_space_constraint(v, pltpu.HBM) for v in (waves, levels, coeffs, angles, order)
    ]
    out, image = pl.pallas_call(
        functools.partial(kernel, sizes),
        out_shape=(jax.ShapeDtypeStruct(shape, f32), jax.ShapeDtypeStruct(image_shape, f32)),
        in_specs=[hbm] * 5,
        out_specs=(vmem, vmem),
        scratch_shapes=[
            pltpu.SMEM(order.shape, jnp.int32),
            pltpu.VMEM(levels_shape, jnp.int32),
            pltpu.VMEM(coeffs_shape, f32),
            pltpu.VMEM(angles_shape, f32),
            pltpu.SemaphoreType.DMA((4 + freqs,)),
            pltpu.VMEM((LANES, LANES), jnp.int32),
            pltpu.VMEM((2, level_count, coeffs_shape[2], LANES), f32),
            pltpu.VMEM((2, angles_shape[0], LANES), f32),
            pltpu.VMEM((freqs,) + table, bf16),
            pltpu.VMEM((freqs, rows, cells), f32),
            pltpu.VMEM((freqs, rows, cells), f32),
            pltpu.VMEM((freqs, 2, 2, rows, cells), f32),
            pltpu.VMEM((2, 2, LANES + 2 * half, 2 * LANES), bf16),
            pltpu.VMEM((2, LANES, 2 * LANES), f32),
            pltpu.VMEM((STEPS, freqs, 2, 2, span, cells), f32),
            pltpu.VMEM((2, 2, 2, span, cells), bf16),
            pltpu.SemaphoreType.DMA((STEPS, freqs, 2)),
            pltpu.SemaphoreType.DMA((STEPS, freqs, 2)),
        ],
        compiler_params=pltpu.CompilerParams(
            collective_id=0, has_side_effects=True, vmem_limit_bytes=32 * 1024 * 1024
        ),
    )(waves, levels, coeffs, angles, order)
    return pl.pallas_call(
        store_kernel,
        out_shape=(jax.ShapeDtypeStruct(shape, f32), jax.ShapeDtypeStruct(image_shape, f32)),
        in_specs=[vmem, vmem],
        out_specs=(hbm, hbm),
        scratch_shapes=[pltpu.SemaphoreType.DMA((2,))],
        compiler_params=pltpu.CompilerParams(vmem_limit_bytes=8 * 1024 * 1024),
    )(out, image)


def solution(mesh):
    in_specs = (P(None, None, "shot", "strip", None), P("strip", None), P(), P(), P("shot"))
    out_specs = (P(None, None, "shot", "strip", None), P("shot", "strip", None))
    return jax.shard_map(
        functools.partial(on_device, mesh.shape["strip"]),
        mesh=mesh,
        in_specs=in_specs,
        out_specs=out_specs,
        check_vma=False,
    )
```

```python
import functools

import jax
import jax.numpy as jnp
from jax import lax
from jax.experimental import pallas as pl
from jax.experimental.pallas import tpu as pltpu
from jax.sharding import PartitionSpec as P

STEPS = 2
LANES = 128
SUBS = 8
WIN = 16
RAW = 1
MESH = pl.DeviceIdType.MESH


def split(v):
    high = v.astype(jnp.bfloat16)
    low = (v - high.astype(jnp.float32)).astype(jnp.bfloat16)
    return high, low


def pick(level, entries):
    out = entries[0]
    for i, entry in enumerate(entries[1:], 1):
        out = jnp.where(level == i, entry, out)
    return out


def filtered(table, parts, level):
    (hr, hi), (lr, li) = parts
    sums = jnp.dot(
        table, jnp.concatenate([hr, hi, lr, li, hr, hi], axis=0), preferred_element_type=jnp.float32
    )
    count = sums.shape[0] // (2 * WIN)
    return [
        pick(level, [sums[(2 * i + comp) * WIN : (2 * i + comp + 1) * WIN] for i in range(count)])
        for comp in range(2)
    ]


def kernel(
    sizes, waves_hbm, levels_hbm, coeffs_hbm, angles_hbm, order_hbm, out_ref, image_ref,
    order_ref, level_ref, coef_ref, angle_ref, load_sem,
    turned_ref, base_ref, turn_ref, table_ref, cos_ref, sin_ref,
    field_ref, part_ref, pass_ref, mid_ref, cross_ref, send_sem, recv_sem,
    edge_level_ref, edge_turned_ref, edge_ref, edge_part_ref, edge_pass_ref, raw_send_sem, raw_recv_sem,
):
    freqs, rows, cells, levels, taps, strips = sizes
    half = taps // 2
    blocks = cells // LANES
    me = lax.axis_index("strip")
    has_low, has_high = me > 0, me < strips - 1

    def neighbour(step):
        return {"strip": me + step}

    barrier = pltpu.get_barrier_semaphore()
    for there, step in ((has_low, -1), (has_high, 1)):

        @pl.when(there)
        def _():
            pl.semaphore_signal(barrier, inc=1, device_id=neighbour(step), device_id_type=MESH)

    small = [
        pltpu.make_async_copy(source, target, load_sem.at[i])
        for i, (source, target) in enumerate(
            ((coeffs_hbm, coef_ref), (angles_hbm, angle_ref), (levels_hbm, level_ref), (order_hbm, order_ref))
        )
    ]
    def wave_load(f):
        return pltpu.make_async_copy(waves_hbm.at[:, :, f], field_ref.at[f], load_sem.at[4 + f])

    early = lax.rem(me, 2) == 0
    skip = jnp.where(early, RAW, 0)

    def turn_of(i):
        return lax.rem(i + skip, freqs)

    def raw_copy(f):
        if f is None:
            source, target, at = levels_hbm.at[pl.ds(0, half), :], edge_level_ref, 0
        else:
            source, target, at = waves_hbm.at[:, :, f, pl.ds(0, half), :], edge_ref.at[f], f + 1
        return pltpu.make_async_remote_copy(
            src_ref=source,
            dst_ref=target,
            send_sem=raw_send_sem.at[at],
            recv_sem=raw_recv_sem.at[at],
            device_id=neighbour(-1),
            device_id_type=MESH,
        )

    def enter():
        pl.semaphore_wait(barrier, has_low.astype(jnp.int32) + has_high.astype(jnp.int32))

    sends_raw = jnp.logical_and(early, has_low)
    gets_raw = jnp.logical_and(jnp.logical_not(early), has_high)

    @pl.when(early)
    def _():
        enter()

    @pl.when(sends_raw)
    def _():
        for f in [*range(RAW), None]:
            raw_copy(f).start()

    wave_load(turn_of(0)).start()
    for load in small:
        load.start()

    for i in range(1, freqs):
        wave_load(turn_of(i)).start()

    lane = lax.broadcasted_iota(jnp.int32, (SUBS, LANES), 1)

    for there, first in ((has_low, 0), (has_high, rows + half)):

        @pl.when(jnp.logical_not(there))
        def _():
            for step in range(STEPS):

                @pl.loop(0, freqs)
                def _(f):
                    for field in range(2):
                        for comp in range(2):
                            mid_ref[step, f, field, comp, first : first + half, :] = jnp.zeros(
                                (half, cells), jnp.float32
                            )

    base_ref[...] = jnp.zeros_like(base_ref)
    small[0].wait()
    for comp in range(2):
        for level in range(levels):
            base_ref[comp, level, :, :taps] = coef_ref[comp, level]
    for level in range(levels):
        real, imag = base_ref[0, level], base_ref[1, level]
        for comp, (first, second) in enumerate(((real, -imag), (imag, real))):
            both = first + pltpu.roll(second, 2 * WIN, 1)
            base_ref[comp, level] = both + pltpu.roll(both, 4 * WIN, 1)

    small[1].wait()
    turn_ref[...] = jnp.zeros_like(turn_ref)
    angle = angle_ref[...]
    turn_ref[0, :, :levels] = jnp.cos(angle)
    turn_ref[1, :, :levels] = jnp.sin(angle)

    small[2].wait()
    small[3].wait()
    stacked = jnp.concatenate([level_ref[:, q * LANES : (q + 1) * LANES] for q in range(blocks)], axis=0)
    turned_ref[...] = stacked.T

    def stack(v):
        return jnp.concatenate([v[:, q * LANES : (q + 1) * LANES] for q in range(blocks)], axis=0)

    def margins(v, count, width):
        place = lax.rem(lane, width)
        before = jnp.where(place >= count, pltpu.roll(v[LANES - half :], count, 1), 0.0)
        after = jnp.where(place < width - count, pltpu.roll(v[:half], LANES - count, 1), 0.0)
        return jnp.concatenate([before, v, after], axis=0)

    def turn_entries(which, f):
        line = turn_ref[which, pl.ds(order_ref[f], 1), :]
        return [jnp.broadcast_to(line[:, i : i + 1], (SUBS, LANES)) for i in range(levels)]

    def edge_pass(f):
        level = stack(edge_level_ref[...])
        cosine, sine = [
            pick(level, [jnp.concatenate([e] * blocks, axis=0) for e in turn_entries(which, f)]) for which in range(2)
        ]
        reals, imags = [], []
        for field in range(2):
            real, imag = [stack(edge_ref[f, field, comp]) for comp in range(2)]
            if field == 1:
                imag = -imag
            reals.append(real * cosine - imag * sine)
            imags.append(real * sine + imag * cosine)
        v = margins(jnp.concatenate(reals + imags, axis=0).T, half, LANES // 4)
        for comp, u in enumerate((v, pltpu.roll(v, LANES // 2, 1))):
            for part, piece in enumerate(split(u)):
                edge_part_ref[part, comp] = piece
        table = table_ref[f]
        low_lanes = lax.broadcasted_iota(jnp.int32, (WIN, LANES), 1) < LANES // 2
        for b in range(0, LANES, WIN):
            parts = [[edge_part_ref[part, comp, b : b + 2 * WIN, :] for comp in range(2)] for part in range(2)]
            real, imag = filtered(table, parts, edge_turned_ref[b : b + WIN, :])
            edge_pass_ref[b : b + WIN, :] = jnp.where(low_lanes, real, pltpu.roll(imag, LANES // 2, 1))
        v = edge_pass_ref[...].T
        for comp in range(2):
            for field in range(2):
                for q in range(blocks):
                    at = ((comp * 2 + field) * blocks + q) * half
                    mid_ref[0, f, field, comp, half + rows :, q * LANES : (q + 1) * LANES] = v[at : at + half]

    def prepare(f):
        row = pl.ds(order_ref[f], 1)
        for level in range(levels):
            for comp in range(2):
                line = jnp.broadcast_to(base_ref[comp, level, row, :], (WIN, LANES))
                high, low = split(pltpu.roll(line, 0, 1, stride=1, stride_axis=0))
                at = (2 * level + comp) * WIN
                table_ref[f, at : at + WIN, :LANES] = high
                table_ref[f, at : at + WIN, LANES:] = low[:, : 4 * WIN]
        for which, target in enumerate((cos_ref, sin_ref)):
            entries = turn_entries(which, f)
            for top in range(0, rows, SUBS):
                for q in range(blocks):
                    level = level_ref[top : top + SUBS, q * LANES : (q + 1) * LANES]
                    target[f, top : top + SUBS, q * LANES : (q + 1) * LANES] = pick(level, entries)

    def inline_pass(step, f):
        cosine, sine = cos_ref[f], sin_ref[f]
        for field in range(2):
            real, imag = field_ref[f, field, 0], field_ref[f, field, 1]
            if step == 0 and field == 1:
                imag = -imag
            turned = (real * cosine - imag * sine, real * sine + imag * cosine)
            for comp in range(2):
                v = turned[comp]
                v = jnp.concatenate([v[:, q * LANES : (q + 1) * LANES] for q in range(blocks)], axis=0).T
                before = jnp.where(lane >= rows, pltpu.roll(v[LANES - half :], rows, 1), 0.0)
                after = jnp.where(lane < LANES - rows, pltpu.roll(v[:half], LANES - rows, 1), 0.0)
                for part, piece in enumerate(split(jnp.concatenate([before, v, after], axis=0))):
                    part_ref[part, comp, :, field * LANES : (field + 1) * LANES] = piece
        table = table_ref[f]
        for b in range(0, LANES, WIN):
            parts = [[part_ref[part, comp, b : b + 2 * WIN, :] for comp in range(2)] for part in range(2)]
            level = turned_ref[b : b + WIN, :]
            sums = filtered(table, parts, jnp.concatenate([level, level], axis=1))
            for comp in range(2):
                pass_ref[comp, b : b + WIN, :] = sums[comp]
        for field in range(2):
            for comp in range(2):
                v = pass_ref[comp, :, field * LANES : (field + 1) * LANES].T
                for q in range(blocks):
                    mid_ref[step, f, field, comp, half : half + rows, q * LANES : (q + 1) * LANES] = v[
                        q * rows : (q + 1) * rows
                    ]

    def cross_pass(step, f):
        last = step == STEPS - 1
        for field in range(2):
            for comp in range(2):
                for part, piece in enumerate(split(mid_ref[step, f, field, comp])):
                    cross_ref[part, field, comp] = piece
        table = table_ref[f]
        wide = 2 * LANES
        for b in range(0, rows, WIN):
            for x in range(0, cells, wide):
                at = (slice(b, b + WIN), slice(x, x + wide))
                level = level_ref[at]
                sums = []
                for field in range(2):
                    parts = [
                        [cross_ref[part, field, comp, b : b + 2 * WIN, x : x + wide] for comp in range(2)]
                        for part in range(2)
                    ]
                    sums.append(filtered(table, parts, level))
                (sr, si), (qr, qi) = sums
                for field in range(2):
                    for comp in range(2):
                        v = sums[field][comp]
                        if last:
                            out_ref[(field, comp, f) + at] = -v if field and comp else v
                        else:
                            field_ref[(f, field, comp) + at] = v
                image_ref[(step,) + at] += sr * qr - si * qi

    def halo_copy(step, f, side):
        source, target = ((half, rows + half), (rows, 0))[side]
        return pltpu.make_async_remote_copy(
            src_ref=mid_ref.at[step, f, :, :, pl.ds(source, half), :],
            dst_ref=mid_ref.at[step, f, :, :, pl.ds(target, half), :],
            send_sem=send_sem.at[step, f, side],
            recv_sem=recv_sem.at[step, f, side],
            device_id=neighbour((-1, 1)[side]),
            device_id_type=MESH,
        )

    def outgoing(step, f):
        if step == 0:
            return jnp.logical_and(has_low, jnp.logical_or(jnp.logical_not(early), f >= RAW)), has_high
        return has_low, has_high

    def incoming(step, f):
        if step == 0:
            return has_low, jnp.logical_and(has_high, jnp.logical_or(early, f >= RAW))
        return has_low, has_high

    def send(step, f):
        for side, there in enumerate(outgoing(step, f)):

            @pl.when(there)
            def _():
                halo_copy(step, f, side).start()

    def receive(step, f):
        for side, there in enumerate(incoming(step, f)):

            @pl.when(there)
            def _():
                halo_copy(step, f, 1 - side).wait_recv()

    image_ref[...] = jnp.zeros_like(image_ref)

    @pl.loop(0, freqs)
    def _(i):
        f = turn_of(i)
        prepare(f)
        wave_load(f).wait()
        inline_pass(0, f)

        @pl.when(jnp.logical_and(i == 0, jnp.logical_not(early)))
        def _():
            enter()

        send(0, f)

    @pl.when(gets_raw)
    def _():
        raw_copy(None).wait_recv()
        edge = stack(edge_level_ref[...])
        edge_turned_ref[...] = jnp.concatenate([edge] * 4, axis=0).T

        @pl.loop(0, RAW)
        def _(f):
            raw_copy(f).wait_recv()
            edge_pass(f)

    @pl.loop(0, freqs)
    def _(f):
        receive(0, f)
        cross_pass(0, f)
        inline_pass(1, f)
        send(1, f)

    @pl.loop(0, freqs)
    def _(f):
        receive(1, f)
        cross_pass(1, f)

    @pl.when(sends_raw)
    def _():
        for f in [*range(RAW), None]:
            raw_copy(f).wait_send()

    for step in range(STEPS):

        @pl.loop(0, freqs)
        def _(f):
            for side, there in enumerate(outgoing(step, f)):

                @pl.when(there)
                def _():
                    halo_copy(step, f, side).wait_send()


def store_kernel(waves_ref, image_ref, waves_hbm, image_hbm, sem):
    copies = [
        pltpu.make_async_copy(waves_ref, waves_hbm, sem.at[0]),
        pltpu.make_async_copy(image_ref, image_hbm, sem.at[1]),
    ]
    for copy in copies:
        copy.start()
    for copy in copies:
        copy.wait()


def on_device(strips, waves, levels, coeffs, angles, order):
    freqs, rows, cells = waves.shape[2:]
    level_count, taps = coeffs.shape[2:]
    half = taps // 2
    blocks = cells // LANES
    assert blocks * rows == LANES and rows % WIN == 0 and half == SUBS and taps == WIN + 1
    sizes = (freqs, rows, cells, level_count, taps, strips)
    table = (level_count * 2 * WIN, 6 * 2 * WIN)
    coeffs = jnp.transpose(coeffs, (0, 2, 1, 3))
    vmem, hbm = [pl.BlockSpec(memory_space=space) for space in (pltpu.VMEM, pltpu.HBM)]
    f32, bf16 = jnp.float32, jnp.bfloat16
    image_shape = (STEPS, rows, cells)
    span = rows + 2 * half
    shape, levels_shape, coeffs_shape, angles_shape = waves.shape, levels.shape, coeffs.shape, angles.shape
    waves, levels, coeffs, angles, order = [
        pltpu.with_memory_space_constraint(v, pltpu.HBM) for v in (waves, levels, coeffs, angles, order)
    ]
    out, image = pl.pallas_call(
        functools.partial(kernel, sizes),
        out_shape=(jax.ShapeDtypeStruct(shape, f32), jax.ShapeDtypeStruct(image_shape, f32)),
        in_specs=[hbm] * 5,
        out_specs=(vmem, vmem),
        scratch_shapes=[
            pltpu.SMEM(order.shape, jnp.int32),
            pltpu.VMEM(levels_shape, jnp.int32),
            pltpu.VMEM(coeffs_shape, f32),
            pltpu.VMEM(angles_shape, f32),
            pltpu.SemaphoreType.DMA((4 + freqs,)),
            pltpu.VMEM((LANES, LANES), jnp.int32),
            pltpu.VMEM((2, level_count, coeffs_shape[2], LANES), f32),
            pltpu.VMEM((2, angles_shape[0], LANES), f32),
            pltpu.VMEM((freqs,) + table, bf16),
            pltpu.VMEM((freqs, rows, cells), f32),
            pltpu.VMEM((freqs, rows, cells), f32),
            pltpu.VMEM((freqs, 2, 2, rows, cells), f32),
            pltpu.VMEM((2, 2, LANES + 2 * half, 2 * LANES), bf16),
            pltpu.VMEM((2, LANES, 2 * LANES), f32),
            pltpu.VMEM((STEPS, freqs, 2, 2, span, cells), f32),
            pltpu.VMEM((2, 2, 2, span, cells), bf16),
            pltpu.SemaphoreType.DMA((STEPS, freqs, 2)),
            pltpu.SemaphoreType.DMA((STEPS, freqs, 2)),
            pltpu.VMEM((half, cells), jnp.int32),
            pltpu.VMEM((LANES, LANES), jnp.int32),
            pltpu.VMEM((RAW, 2, 2, half, cells), f32),
            pltpu.VMEM((2, 2, LANES + 2 * half, LANES), bf16),
            pltpu.VMEM((LANES, LANES), f32),
            pltpu.SemaphoreType.DMA((RAW + 1,)),
            pltpu.SemaphoreType.DMA((RAW + 1,)),
        ],
        compiler_params=pltpu.CompilerParams(
            collective_id=0, has_side_effects=True, vmem_limit_bytes=32 * 1024 * 1024
        ),
    )(waves, levels, coeffs, angles, order)
    return pl.pallas_call(
        store_kernel,
        out_shape=(jax.ShapeDtypeStruct(shape, f32), jax.ShapeDtypeStruct(image_shape, f32)),
        in_specs=[vmem, vmem],
        out_specs=(hbm, hbm),
        scratch_shapes=[pltpu.SemaphoreType.DMA((2,))],
        compiler_params=pltpu.CompilerParams(vmem_limit_bytes=8 * 1024 * 1024),
    )(out, image)


def solution(mesh):
    in_specs = (P(None, None, "shot", "strip", None), P("strip", None), P(), P(), P("shot"))
    out_specs = (P(None, None, "shot", "strip", None), P("shot", "strip", None))
    return jax.shard_map(
        functools.partial(on_device, mesh.shape["strip"]),
        mesh=mesh,
        in_specs=in_specs,
        out_specs=out_specs,
        check_vma=False,
    )
```

```python
import functools

import jax
import jax.numpy as jnp
from jax import lax
from jax.experimental import pallas as pl
from jax.experimental.pallas import tpu as pltpu
from jax.sharding import PartitionSpec as P

STEPS = 2
LANES = 128
SUBS = 8
WIN = 16
RAW = 1
MESH = pl.DeviceIdType.MESH


def split(v):
    high = v.astype(jnp.bfloat16)
    low = (v - high.astype(jnp.float32)).astype(jnp.bfloat16)
    return high, low


def pick(level, entries):
    out = entries[0]
    for i, entry in enumerate(entries[1:], 1):
        out = jnp.where(level == i, entry, out)
    return out


def filtered(table, parts, level):
    (hr, hi), (lr, li) = parts
    sums = jnp.dot(
        table, jnp.concatenate([hr, hi, lr, li, hr, hi], axis=0), preferred_element_type=jnp.float32
    )
    count = sums.shape[0] // (2 * WIN)
    return [
        pick(level, [sums[(2 * i + comp) * WIN : (2 * i + comp + 1) * WIN] for i in range(count)])
        for comp in range(2)
    ]


def cross_window(table, level_ref, cross_ref, first, store):
    wide = 2 * LANES
    for x in range(0, level_ref.shape[1], wide):
        at = (pl.ds(first, WIN), slice(x, x + wide))
        level = level_ref[at]
        sums = []
        for field in range(2):
            parts = [
                [cross_ref[part, field, comp, pl.ds(first, 2 * WIN), x : x + wide] for comp in range(2)]
                for part in range(2)
            ]
            sums.append(filtered(table, parts, level))
        store(at, sums)


def windows(me, rows):
    late = lax.rem(me, 2) * (rows - WIN)
    return [pl.multiple_of(first, WIN) for first in (rows - WIN - late, late)]


def kernel(
    sizes, waves_hbm, levels_hbm, coeffs_hbm, angles_hbm, order_hbm,
    out_ref, image_ref, table_ref, level_ref, cross_ref,
    order_ref, coef_ref, angle_ref, load_sem,
    turned_ref, base_ref, turn_ref, cos_ref, sin_ref,
    field_ref, part_ref, pass_ref, mid_ref, send_sem, recv_sem,
    edge_level_ref, edge_turned_ref, edge_ref, edge_part_ref, edge_pass_ref, raw_send_sem, raw_recv_sem,
):
    freqs, rows, cells, levels, taps, strips = sizes
    half = taps // 2
    blocks = cells // LANES
    me = lax.axis_index("strip")
    has_low, has_high = me > 0, me < strips - 1

    def neighbour(step):
        return {"strip": me + step}

    barrier = pltpu.get_barrier_semaphore()
    for there, step in ((has_low, -1), (has_high, 1)):

        @pl.when(there)
        def _():
            pl.semaphore_signal(barrier, inc=1, device_id=neighbour(step), device_id_type=MESH)

    small = [
        pltpu.make_async_copy(source, target, load_sem.at[i])
        for i, (source, target) in enumerate(
            ((coeffs_hbm, coef_ref), (angles_hbm, angle_ref), (levels_hbm, level_ref), (order_hbm, order_ref))
        )
    ]
    def wave_load(f):
        return pltpu.make_async_copy(waves_hbm.at[:, :, f], field_ref.at[f], load_sem.at[4 + f])

    early = lax.rem(me, 2) == 0
    skip = jnp.where(early, RAW, 0)

    def turn_of(i):
        return lax.rem(i + skip, freqs)

    def raw_copy(f):
        if f is None:
            source, target, at = levels_hbm.at[pl.ds(0, half), :], edge_level_ref, 0
        else:
            source, target, at = waves_hbm.at[:, :, f, pl.ds(0, half), :], edge_ref.at[f], f + 1
        return pltpu.make_async_remote_copy(
            src_ref=source,
            dst_ref=target,
            send_sem=raw_send_sem.at[at],
            recv_sem=raw_recv_sem.at[at],
            device_id=neighbour(-1),
            device_id_type=MESH,
        )

    def enter():
        pl.semaphore_wait(barrier, has_low.astype(jnp.int32) + has_high.astype(jnp.int32))

    sends_raw = jnp.logical_and(early, has_low)
    gets_raw = jnp.logical_and(jnp.logical_not(early), has_high)

    @pl.when(early)
    def _():
        enter()

    @pl.when(sends_raw)
    def _():
        for f in [*range(RAW), None]:
            raw_copy(f).start()

    wave_load(turn_of(0)).start()
    for load in small:
        load.start()

    for i in range(1, freqs):
        wave_load(turn_of(i)).start()

    lane = lax.broadcasted_iota(jnp.int32, (SUBS, LANES), 1)

    for there, first in ((has_low, 0), (has_high, rows + half)):

        @pl.when(jnp.logical_not(there))
        def _():
            for step in range(STEPS):

                @pl.loop(0, freqs)
                def _(f):
                    for field in range(2):
                        for comp in range(2):
                            mid_ref[step, f, field, comp, first : first + half, :] = jnp.zeros(
                                (half, cells), jnp.float32
                            )

    base_ref[...] = jnp.zeros_like(base_ref)
    small[0].wait()
    for comp in range(2):
        for level in range(levels):
            base_ref[comp, level, :, :taps] = coef_ref[comp, level]
    for level in range(levels):
        real, imag = base_ref[0, level], base_ref[1, level]
        for comp, (first, second) in enumerate(((real, -imag), (imag, real))):
            both = first + pltpu.roll(second, 2 * WIN, 1)
            base_ref[comp, level] = both + pltpu.roll(both, 4 * WIN, 1)

    small[1].wait()
    turn_ref[...] = jnp.zeros_like(turn_ref)
    angle = angle_ref[...]
    turn_ref[0, :, :levels] = jnp.cos(angle)
    turn_ref[1, :, :levels] = jnp.sin(angle)

    small[2].wait()
    small[3].wait()
    stacked = jnp.concatenate([level_ref[:, q * LANES : (q + 1) * LANES] for q in range(blocks)], axis=0)
    turned_ref[...] = stacked.T

    def stack(v):
        return jnp.concatenate([v[:, q * LANES : (q + 1) * LANES] for q in range(blocks)], axis=0)

    def margins(v, count, width):
        place = lax.rem(lane, width)
        before = jnp.where(place >= count, pltpu.roll(v[LANES - half :], count, 1), 0.0)
        after = jnp.where(place < width - count, pltpu.roll(v[:half], LANES - count, 1), 0.0)
        return jnp.concatenate([before, v, after], axis=0)

    def turn_entries(which, f):
        line = turn_ref[which, pl.ds(order_ref[f], 1), :]
        return [jnp.broadcast_to(line[:, i : i + 1], (SUBS, LANES)) for i in range(levels)]

    def edge_pass(f):
        level = stack(edge_level_ref[...])
        cosine, sine = [
            pick(level, [jnp.concatenate([e] * blocks, axis=0) for e in turn_entries(which, f)]) for which in range(2)
        ]
        reals, imags = [], []
        for field in range(2):
            real, imag = [stack(edge_ref[f, field, comp]) for comp in range(2)]
            if field == 1:
                imag = -imag
            reals.append(real * cosine - imag * sine)
            imags.append(real * sine + imag * cosine)
        v = margins(jnp.concatenate(reals + imags, axis=0).T, half, LANES // 4)
        for comp, u in enumerate((v, pltpu.roll(v, LANES // 2, 1))):
            for part, piece in enumerate(split(u)):
                edge_part_ref[part, comp] = piece
        table = table_ref[f]
        low_lanes = lax.broadcasted_iota(jnp.int32, (WIN, LANES), 1) < LANES // 2
        for b in range(0, LANES, WIN):
            parts = [[edge_part_ref[part, comp, b : b + 2 * WIN, :] for comp in range(2)] for part in range(2)]
            real, imag = filtered(table, parts, edge_turned_ref[b : b + WIN, :])
            edge_pass_ref[b : b + WIN, :] = jnp.where(low_lanes, real, pltpu.roll(imag, LANES // 2, 1))
        v = edge_pass_ref[...].T
        for comp in range(2):
            for field in range(2):
                for q in range(blocks):
                    at = ((comp * 2 + field) * blocks + q) * half
                    mid_ref[0, f, field, comp, half + rows :, q * LANES : (q + 1) * LANES] = v[at : at + half]

    def prepare(f):
        row = pl.ds(order_ref[f], 1)
        for level in range(levels):
            for comp in range(2):
                line = jnp.broadcast_to(base_ref[comp, level, row, :], (WIN, LANES))
                high, low = split(pltpu.roll(line, 0, 1, stride=1, stride_axis=0))
                at = (2 * level + comp) * WIN
                table_ref[f, at : at + WIN, :LANES] = high
                table_ref[f, at : at + WIN, LANES:] = low[:, : 4 * WIN]
        for which, target in enumerate((cos_ref, sin_ref)):
            entries = turn_entries(which, f)
            for top in range(0, rows, SUBS):
                for q in range(blocks):
                    level = level_ref[top : top + SUBS, q * LANES : (q + 1) * LANES]
                    target[f, top : top + SUBS, q * LANES : (q + 1) * LANES] = pick(level, entries)

    def inline_pass(step, f):
        cosine, sine = cos_ref[f], sin_ref[f]
        for field in range(2):
            real, imag = field_ref[f, field, 0], field_ref[f, field, 1]
            if step == 0 and field == 1:
                imag = -imag
            turned = (real * cosine - imag * sine, real * sine + imag * cosine)
            for comp in range(2):
                v = turned[comp]
                v = jnp.concatenate([v[:, q * LANES : (q + 1) * LANES] for q in range(blocks)], axis=0).T
                before = jnp.where(lane >= rows, pltpu.roll(v[LANES - half :], rows, 1), 0.0)
                after = jnp.where(lane < LANES - rows, pltpu.roll(v[:half], LANES - rows, 1), 0.0)
                for part, piece in enumerate(split(jnp.concatenate([before, v, after], axis=0))):
                    part_ref[part, comp, :, field * LANES : (field + 1) * LANES] = piece
        table = table_ref[f]
        for b in range(0, LANES, WIN):
            parts = [[part_ref[part, comp, b : b + 2 * WIN, :] for comp in range(2)] for part in range(2)]
            level = turned_ref[b : b + WIN, :]
            sums = filtered(table, parts, jnp.concatenate([level, level], axis=1))
            for comp in range(2):
                pass_ref[comp, b : b + WIN, :] = sums[comp]
        for field in range(2):
            for comp in range(2):
                v = pass_ref[comp, :, field * LANES : (field + 1) * LANES].T
                for q in range(blocks):
                    mid_ref[step, f, field, comp, half : half + rows, q * LANES : (q + 1) * LANES] = v[
                        q * rows : (q + 1) * rows
                    ]

    def split_rows(step, f, first, count):
        for field in range(2):
            for comp in range(2):
                for part, piece in enumerate(split(mid_ref[step, f, field, comp, pl.ds(first, count), :])):
                    cross_ref[part, field, comp, pl.ds(first, count), :] = piece

    def cross_rows(step, f, first):
        def store(at, sums):
            (sr, si), (qr, qi) = sums
            for field in range(2):
                for comp in range(2):
                    v = sums[field][comp]
                    if step == STEPS - 1:
                        out_ref[(field, comp, f) + at] = -v if field and comp else v
                    else:
                        field_ref[(f, field, comp) + at] = v
            image_ref[(step,) + at] += sr * qr - si * qi

        cross_window(table_ref[f], level_ref, cross_ref, first, store)

    def cross_pass(step, f):
        split_rows(step, f, 0, rows + 2 * half)
        for first in range(0, rows, WIN):
            cross_rows(step, f, first)

    def halo_copy(step, f, side):
        source, target = ((half, rows + half), (rows, 0))[side]
        return pltpu.make_async_remote_copy(
            src_ref=mid_ref.at[step, f, :, :, pl.ds(source, half), :],
            dst_ref=mid_ref.at[step, f, :, :, pl.ds(target, half), :],
            send_sem=send_sem.at[step, f, side],
            recv_sem=recv_sem.at[step, f, side],
            device_id=neighbour((-1, 1)[side]),
            device_id_type=MESH,
        )

    def outgoing(step, f):
        if step == 0:
            return jnp.logical_and(has_low, jnp.logical_or(jnp.logical_not(early), f >= RAW)), has_high
        return has_low, has_high

    def incoming(step, f):
        if step == 0:
            return has_low, jnp.logical_and(has_high, jnp.logical_or(early, f >= RAW))
        return has_low, has_high

    def send(step, f):
        for side, there in enumerate(outgoing(step, f)):

            @pl.when(there)
            def _():
                halo_copy(step, f, side).start()

    def receive(step, f, which=None):
        for side, there in enumerate(incoming(step, f)):
            if which is not None:
                there = jnp.logical_and(there, which[side])

            @pl.when(there)
            def _():
                halo_copy(step, f, 1 - side).wait_recv()

    image_ref[...] = jnp.zeros_like(image_ref)

    @pl.loop(0, freqs)
    def _(i):
        f = turn_of(i)
        prepare(f)
        wave_load(f).wait()
        inline_pass(0, f)

        @pl.when(jnp.logical_and(i == 0, jnp.logical_not(early)))
        def _():
            enter()

        send(0, f)

    @pl.when(gets_raw)
    def _():
        raw_copy(None).wait_recv()
        edge = stack(edge_level_ref[...])
        edge_turned_ref[...] = jnp.concatenate([edge] * 4, axis=0).T

        @pl.loop(0, RAW)
        def _(f):
            raw_copy(f).wait_recv()
            edge_pass(f)

    @pl.loop(0, freqs)
    def _(f):
        receive(0, f)
        cross_pass(0, f)
        inline_pass(1, f)
        send(1, f)

    @pl.loop(0, freqs - 1)
    def _(f):
        receive(1, f)
        cross_pass(1, f)

    soon, late = windows(me, rows)
    receive(1, freqs - 1, (jnp.logical_not(early), early))
    split_rows(1, freqs - 1, soon, 2 * WIN)
    cross_rows(1, freqs - 1, soon)
    receive(1, freqs - 1, (early, jnp.logical_not(early)))
    split_rows(1, freqs - 1, late, 2 * WIN)

    @pl.when(sends_raw)
    def _():
        for f in [*range(RAW), None]:
            raw_copy(f).wait_send()

    for step in range(STEPS):

        @pl.loop(0, freqs)
        def _(f):
            for side, there in enumerate(outgoing(step, f)):

                @pl.when(there)
                def _():
                    halo_copy(step, f, side).wait_send()


def store_kernel(waves_ref, image_ref, table_ref, level_ref, cross_ref, waves_hbm, image_hbm, last_ref, sum_ref, sem):
    freqs, rows = waves_ref.shape[2:4]
    soon, late = windows(lax.axis_index("strip"), rows)
    done, step = freqs - 1, image_ref.shape[0] - 1
    early, after = pl.ds(soon, WIN), pl.ds(late, WIN)
    copies = [
        pltpu.make_async_copy(source, target, sem.at[i])
        for i, (source, target) in enumerate(
            (
                (waves_ref.at[:, :, pl.ds(0, done)], waves_hbm.at[:, :, pl.ds(0, done)]),
                (image_ref.at[pl.ds(0, step)], image_hbm.at[pl.ds(0, step)]),
                (waves_ref.at[:, :, done, early], waves_hbm.at[:, :, done, early]),
                (image_ref.at[step, early], image_hbm.at[step, early]),
                (last_ref, waves_hbm.at[:, :, done, after]),
                (sum_ref, image_hbm.at[step, after]),
            )
        )
    ]
    for copy in copies[:4]:
        copy.start()

    def store(at, sums):
        (sr, si), (qr, qi) = sums
        for field in range(2):
            for comp in range(2):
                v = sums[field][comp]
                last_ref[field, comp, :, at[1]] = -v if field and comp else v
        sum_ref[:, at[1]] = image_ref[(step,) + at] + sr * qr - si * qi

    cross_window(table_ref[done], level_ref, cross_ref, late, store)
    for copy in copies[4:]:
        copy.start()
    for copy in copies:
        copy.wait()


def on_device(strips, waves, levels, coeffs, angles, order):
    freqs, rows, cells = waves.shape[2:]
    level_count, taps = coeffs.shape[2:]
    half = taps // 2
    blocks = cells // LANES
    assert blocks * rows == LANES and rows == 2 * WIN and half == SUBS and taps == WIN + 1
    sizes = (freqs, rows, cells, level_count, taps, strips)
    table = (level_count * 2 * WIN, 6 * 2 * WIN)
    coeffs = jnp.transpose(coeffs, (0, 2, 1, 3))
    vmem, hbm = [pl.BlockSpec(memory_space=space) for space in (pltpu.VMEM, pltpu.HBM)]
    f32, bf16 = jnp.float32, jnp.bfloat16
    image_shape = (STEPS, rows, cells)
    span = rows + 2 * half
    shape, levels_shape, coeffs_shape, angles_shape = waves.shape, levels.shape, coeffs.shape, angles.shape
    waves, levels, coeffs, angles, order = [
        pltpu.with_memory_space_constraint(v, pltpu.HBM) for v in (waves, levels, coeffs, angles, order)
    ]
    held = (
        jax.ShapeDtypeStruct(shape, f32),
        jax.ShapeDtypeStruct(image_shape, f32),
        jax.ShapeDtypeStruct((freqs,) + table, bf16),
        jax.ShapeDtypeStruct(levels_shape, jnp.int32),
        jax.ShapeDtypeStruct((2, 2, 2, span, cells), bf16),
    )
    held = pl.pallas_call(
        functools.partial(kernel, sizes),
        out_shape=held,
        in_specs=[hbm] * 5,
        out_specs=(vmem,) * len(held),
        scratch_shapes=[
            pltpu.SMEM(order.shape, jnp.int32),
            pltpu.VMEM(coeffs_shape, f32),
            pltpu.VMEM(angles_shape, f32),
            pltpu.SemaphoreType.DMA((4 + freqs,)),
            pltpu.VMEM((LANES, LANES), jnp.int32),
            pltpu.VMEM((2, level_count, coeffs_shape[2], LANES), f32),
            pltpu.VMEM((2, angles_shape[0], LANES), f32),
            pltpu.VMEM((freqs, rows, cells), f32),
            pltpu.VMEM((freqs, rows, cells), f32),
            pltpu.VMEM((freqs, 2, 2, rows, cells), f32),
            pltpu.VMEM((2, 2, LANES + 2 * half, 2 * LANES), bf16),
            pltpu.VMEM((2, LANES, 2 * LANES), f32),
            pltpu.VMEM((STEPS, freqs, 2, 2, span, cells), f32),
            pltpu.SemaphoreType.DMA((STEPS, freqs, 2)),
            pltpu.SemaphoreType.DMA((STEPS, freqs, 2)),
            pltpu.VMEM((half, cells), jnp.int32),
            pltpu.VMEM((LANES, LANES), jnp.int32),
            pltpu.VMEM((RAW, 2, 2, half, cells), f32),
            pltpu.VMEM((2, 2, LANES + 2 * half, LANES), bf16),
            pltpu.VMEM((LANES, LANES), f32),
            pltpu.SemaphoreType.DMA((RAW + 1,)),
            pltpu.SemaphoreType.DMA((RAW + 1,)),
        ],
        compiler_params=pltpu.CompilerParams(
            collective_id=0, has_side_effects=True, vmem_limit_bytes=32 * 1024 * 1024
        ),
    )(waves, levels, coeffs, angles, order)
    return pl.pallas_call(
        store_kernel,
        out_shape=(jax.ShapeDtypeStruct(shape, f32), jax.ShapeDtypeStruct(image_shape, f32)),
        in_specs=[vmem] * len(held),
        out_specs=(hbm, hbm),
        scratch_shapes=[
            pltpu.VMEM((2, 2, WIN, cells), f32),
            pltpu.VMEM((WIN, cells), f32),
            pltpu.SemaphoreType.DMA((6,)),
        ],
        compiler_params=pltpu.CompilerParams(vmem_limit_bytes=8 * 1024 * 1024),
    )(*held)


def solution(mesh):
    in_specs = (P(None, None, "shot", "strip", None), P("strip", None), P(), P(), P("shot"))
    out_specs = (P(None, None, "shot", "strip", None), P("shot", "strip", None))
    return jax.shard_map(
        functools.partial(on_device, mesh.shape["strip"]),
        mesh=mesh,
        in_specs=in_specs,
        out_specs=out_specs,
        check_vma=False,
    )
```
